32 devices in a mesh: grp: 4 (over x, core), tp: 8 (over z, y).
Axes of the slice: x: 2, y: 2, z: 4, core: 2. Of those that a mesh axis runs over, the one named last changes fastest.
Arguments:
- acts: bfloat16 [512, 8192], P('grp', 'tp'), may hold values from -6 to 6
- cotangent: bfloat16 [512, 8192], P('tp', 'grp'), may hold values from -18 to 18
- weight: bfloat16 [8192, 8192], P('tp', 'grp'), may hold values from -0.0625 to 0.0625
- moment: float32 [8192, 8192], P('tp', 'grp'), may hold values from -3 to 3
- second: float32 [8192, 8192], P('tp', 'grp'), may hold values from 0.05 to 1
- roll_acts: bfloat16 [64, 8192], P('grp', 'tp'), may hold values from -6 to 6
- live: int32 [4], P('grp'), may hold values from 4 to 16, as said below
Outputs:
- moment_new: float32 [8192, 8192], P('tp', 'grp')
- second_new: float32 [8192, 8192], P('tp', 'grp')
- prefill_out: bfloat16 [64, 8192], P('grp', 'tp')
The draws below stay inside these ranges and needn't reach their ends.
Inputs may be any that keep to these rules, and one draw needn't show every extreme that they name: live slots of each replica's 16; some replica is full in every draw.
All inputs are finite; a program needn't handle non-finite values.
Results may differ from the reference program's by a relative error of at most 0.023.
Values may be sent and summed in bfloat16 or wider, within the bound.
No kernel may reach another device: no remote copies, remote signals or barrier semaphores. Data moves between devices by JAX's collectives and lax.ppermute only.
A program may use at most 128 MiB of HBM per device.

```python
import math
import jax
import jax.numpy as jnp
from jax import lax

E = 8192
D = 8192
RT = 16
LT = 512
ROLL = 64
N_GRP = 4
N_TP = 8


def draw_live(key, part):
    first, other = jax.random.split(jax.random.fold_in(key, 11))
    counts = jax.random.randint(first, (N_GRP,), RT // 4, RT + 1)
    chosen = jax.random.randint(other, (), 0, N_GRP)
    places = jnp.arange(N_GRP, dtype=jnp.int32)
    return jnp.where(places == chosen, RT, counts).astype(jnp.int32)


def draw_cotangent(key, part):
    inner = jax.random.fold_in(key, 23)
    column = jnp.arange(D, dtype=jnp.float32) / jnp.float32(max(D - 1, 1))
    values = jnp.clip(jax.random.normal(inner, (LT, D), jnp.float32), -6.0, 6.0)
    scaled = values * (1.0 + 2.0 * column)[None, :]
    return scaled.astype(jnp.bfloat16)


def block_scale(rng, extent, cuts, low, top_value):
    def one(position, shards_of):
        heights = jax.random.uniform(jax.random.fold_in(jax.random.fold_in(rng, 6), position), (shards_of,), jnp.float32, low / len(cuts), top_value / len(cuts))
        return jnp.repeat(jnp.exp(heights), extent[position] // shards_of).reshape((-1,) + (1,) * (len(extent) - position - 1))

    gain = one(*cuts[0])
    for cut in cuts[1:]:
        gain = gain * one(*cut)
    return gain


def noise(stream_key, extent, spread, bound, shards=(), kind=jnp.bfloat16):
    level = block_scale(stream_key, extent, shards, -0.22, 0.18) if shards else 1.0
    drawn = jax.random.normal(stream_key, extent, jnp.float32) * spread * level
    return jnp.minimum(jnp.maximum(drawn, -bound), bound).astype(kind)


def setup_inputs(seed: int = 0) -> dict:
    arg_keys = jax.random.split(jax.random.key(seed), 8)
    acts = noise(arg_keys[0], (LT, E), 1.0, 6.0, ((0, 4), (1, 8)))
    cotangent = draw_cotangent(jax.random.fold_in(arg_keys[7], 71), 0)
    weight = noise(arg_keys[2], (E, D), E ** -0.5, 0.0625, ((0, 8), (1, 4)))
    moment = noise(arg_keys[3], (E, D), 0.3, 3.0, ((0, 8), (1, 4)), jnp.float32)
    second = jnp.clip(jnp.exp(math.log(1.0) - 2.9957323 * jax.random.uniform(arg_keys[4], (E, D), jnp.float32) ** block_scale(arg_keys[4], (E, D), ((0, 8), (1, 4)), -0.2, 0.2)), 0.05, 1.0)
    roll_acts = noise(arg_keys[5], (ROLL, E), 1.0, 6.0, ((0, 4), (1, 8)))
    live = draw_live(jax.random.fold_in(arg_keys[7], 71), 0)
    return dict(acts=acts, cotangent=cotangent, weight=weight, moment=moment, second=second, roll_acts=roll_acts, live=live)


beta_one = 0.9
beta_two = 0.95
learn_rate = 0.003
weight_decay = 0.1
adam_eps = 1e-08
step_count = 10

def reference(acts, cotangent, weight, moment, second, roll_acts, live):
    grad = jnp.dot(acts.T, cotangent, preferred_element_type=jnp.float32)
    total_sq = jnp.sum(grad * grad)
    factor = jnp.minimum(1.0, 1.0 / jnp.sqrt(total_sq / (E * D) + 1e-06))
    clipped = grad * factor
    moment_new = beta_one * moment + (1.0 - beta_one) * clipped
    second_new = beta_two * second + (1.0 - beta_two) * clipped * clipped
    m_hat = moment_new / (1.0 - beta_one ** step_count)
    v_hat = second_new / (1.0 - beta_two ** step_count)
    old = weight.astype(jnp.float32)
    weight_new = (old - learn_rate * (m_hat / (jnp.sqrt(v_hat) + adam_eps) + weight_decay * old)).astype(jnp.bfloat16)
    block = E // N_TP
    feats = roll_acts.reshape(ROLL, N_TP, block).transpose(1, 0, 2)
    blocks = weight_new.reshape(N_TP, block, D)

    def accumulate(total, pair):
        piece = jnp.dot(pair[0], pair[1], preferred_element_type=jnp.float32).astype(jnp.bfloat16)
        piece = lax.optimization_barrier(piece)
        return (total + piece.astype(jnp.float32), None)
    projected, _ = lax.scan(accumulate, jnp.zeros((ROLL, D), jnp.float32), (feats, blocks))
    slots = jnp.arange(ROLL, dtype=jnp.int32)
    owners = jnp.repeat(live, RT)
    alive = slots % RT < owners
    prefill_out = jnp.where(alive[:, None], projected, jnp.float32(0.0)).astype(jnp.bfloat16)
    return (moment_new, second_new, prefill_out)
```

```python
import functools

import jax
import jax.numpy as jnp
from jax import lax
from jax.experimental import pallas as pl
from jax.experimental.pallas import tpu as pltpu
from jax.sharding import PartitionSpec as P

E = 8192
D = 8192

beta_one = 0.9
beta_two = 0.95
learn_rate = 0.003
weight_decay = 0.1
adam_eps = 1e-08
step_count = 10

root_two = (1.0 - beta_two**step_count) ** 0.5
step_scale = learn_rate * root_two / (1.0 - beta_one**step_count)
eps_scaled = adam_eps * root_two
keep_scale = 1.0 - learn_rate * weight_decay


MIB = 1024 * 1024
ANY = pl.BlockSpec(memory_space=pl.ANY)
VMEM = pl.BlockSpec(memory_space=pltpu.VMEM)


def ring_order(count):
    return list(range(0, count, 2)) + list(range(1, count, 2))[::-1]


def ring_member(place, count):
    return jnp.where(place < (count + 1) // 2, 2 * place, 2 * (count - 1 - place) + 1)


def ring_place(member, count):
    return jnp.where(member % 2 == 0, member // 2, count - 1 - member // 2)


def ring_gather(block, axis, count):
    order = ring_order(count)
    ahead = [(order[i], order[(i + 1) % count]) for i in range(count)]
    back = [(b, a) for a, b in ahead]
    half = block.shape[0] // 2
    pieces = (block[:half], block[half:])
    out, offsets = [[block]], [0]
    left, right = list(pieces), list(pieces)
    for step in range(1, (count - 1) // 2 + 1):
        moved = []
        for i in range(2):
            moved.append(
                (lax.ppermute(left[i], axis, ahead), lax.ppermute(right[i], axis, back))
            )
        left, right = [m[0] for m in moved], [m[1] for m in moved]
        out += [list(left), list(right)]
        offsets += [-step, step]
    if count % 2 == 0:
        out.append(
            [lax.ppermute(left[0], axis, ahead), lax.ppermute(right[1], axis, back)]
        )
        offsets.append(count // 2)
    return out, offsets


def prep_kernel(offsets, n_grp, n_tp, rows, *refs):
    packs = refs[:n_grp]
    at_ref, roll_ref, held, sems = refs[n_grp:]
    learn = held.shape[0] // n_grp
    slots = roll_ref.shape[0] // n_grp
    me = lax.axis_index("grp")
    copies = []
    for j in range(n_grp):
        owner = lax.rem(me + n_grp - j, n_grp)
        copies.append(
            pltpu.make_async_copy(
                packs[j].at[pl.ds(0, learn), :],
                held.at[pl.ds(pl.multiple_of(owner * learn, learn), learn), :],
                sems.at[2 * j],
            )
        )
        copies.append(
            pltpu.make_async_copy(
                packs[j].at[pl.ds(learn, slots), :],
                roll_ref.at[pl.ds(pl.multiple_of(owner * slots, slots), slots), :],
                sems.at[2 * j + 1],
            )
        )
    for c in copies:
        c.start()
    for c in copies:
        c.wait()
    place = ring_place(lax.axis_index("tp"), n_tp)
    parts = []
    for off in offsets:
        member = ring_member(lax.rem(place + off + n_tp, n_tp), n_tp)
        parts.append(held[pl.ds(pl.multiple_of(member * rows, rows), rows), :])
    at_ref[...] = jnp.concatenate(parts, axis=0).T


def grad_kernel(layout, n_all, tile, *refs):
    n_in = len(layout)
    at_ref = refs[0]
    pieces = refs[1 : 1 + n_in]
    grad_ref, sq_ref, cot, sems = refs[1 + n_in :]
    copies = []
    for i, (start, rows) in enumerate(layout):
        copies.append(
            pltpu.make_async_copy(pieces[i], cot.at[pl.ds(start, rows), :], sems.at[i])
        )
    for c in copies:
        c.start()
    for c in copies:
        c.wait()
    width = grad_ref.shape[1]
    total = jnp.zeros((8, 128), jnp.float32)
    for j in range(width // tile):
        part = jnp.dot(
            at_ref[...],
            cot[:, j * tile : (j + 1) * tile],
            preferred_element_type=jnp.float32,
        )
        grad_ref[:, j * tile : (j + 1) * tile] = part
        squares = part * part
        rows = jnp.sum(squares.reshape(-1, 8, tile), axis=0)
        for k in range(tile // 128):
            total = total + rows[:, k * 128 : (k + 1) * 128]
    for i in range(n_all):
        sq_ref[i * 8 : (i + 1) * 8, :] = total


def update_kernel(
    n_grp, count, sq_ref, grad_ref, moment_ref, second_ref, weight_ref, roll_ref,
    moment_out, second_out, part_ref, fresh, total,
):
    step = pl.program_id(0)
    rows, width = moment_ref.shape
    total_sq = jnp.sum(sq_ref[...])
    ratio = jnp.full((1, 128), total_sq / count + 1e-06, jnp.float32)
    factor = jnp.minimum(1.0, 1.0 / jnp.sqrt(ratio))
    first = jnp.broadcast_to((1.0 - beta_one) * factor, (16, 128))
    other = jnp.broadcast_to((1.0 - beta_two) * factor * factor, (16, 128))
    wide = min(width, 512)
    first = jnp.concatenate([first] * (wide // 128), axis=1)
    other = jnp.concatenate([other] * (wide // 128), axis=1)

    def body(i, _):
        at = pl.ds(pl.multiple_of(i * 16, 16), 16)
        for j in range(width // wide):
            cols = slice(j * wide, (j + 1) * wide)
            grad = grad_ref[at, cols]
            moment = beta_one * moment_ref[at, cols] + first * grad
            second = beta_two * second_ref[at, cols] + (other * grad) * grad
            moment_out[at, cols] = moment
            second_out[at, cols] = second
            root = second * lax.rsqrt(second)
            move = (step_scale * moment) / (root + eps_scaled)
            old = weight_ref[at, cols].astype(jnp.float32)
            fresh[at, cols] = (keep_scale * old - move).astype(jnp.bfloat16)
        return 0

    lax.fori_loop(0, rows // 16, body, 0)
    part = jnp.dot(roll_ref[...], fresh[...], preferred_element_type=jnp.float32)

    @pl.when(step == 0)
    def _():
        total[...] = part

    @pl.when(step > 0)
    def _():
        total[...] += part

    @pl.when(step == pl.num_programs(0) - 1)
    def _():
        out_rows, out_width = part_ref.shape
        slots = roll_ref.shape[0] // n_grp
        halves = width // out_width
        for r in range(n_grp):
            for h in range(halves):
                at = (r * halves + h) * slots
                part_ref[at : at + slots, :] = total[
                    r * slots : (r + 1) * slots, h * out_width : (h + 1) * out_width
                ].astype(jnp.bfloat16)


def shards(n_grp, n_tp, acts, cotangent, weight, moment, second, roll_acts, live):
    n_all = n_grp * n_tp
    feats, width = weight.shape
    slots = roll_acts.shape[0]
    learn = acts.shape[0]
    rows = cotangent.shape[0]
    tokens = rows * n_tp
    both = ("grp", "tp")

    cot_pieces, offsets = ring_gather(cotangent, "tp", n_tp)
    pack = jnp.concatenate([acts, roll_acts], axis=0)
    packs = [pack] + [
        lax.ppermute(pack, "grp", [(i, (i + j) % n_grp) for i in range(n_grp)])
        for j in range(1, n_grp)
    ]
    acts_t, roll_all = pl.pallas_call(
        functools.partial(prep_kernel, offsets, n_grp, n_tp, rows),
        out_shape=(
            jax.ShapeDtypeStruct((feats, tokens), jnp.bfloat16),
            jax.ShapeDtypeStruct((slots * n_grp, feats), jnp.bfloat16),
        ),
        in_specs=[ANY] * n_grp,
        out_specs=(VMEM, VMEM),
        scratch_shapes=[
            pltpu.VMEM((tokens, feats), jnp.bfloat16),
            pltpu.SemaphoreType.DMA((2 * n_grp,)),
        ],
        name="prep",
    )(*packs)

    flat, layout, at = [], [], 0
    for group in cot_pieces:
        for piece in group:
            flat.append(piece)
            layout.append((at, piece.shape[0]))
            at += piece.shape[0]
    tile = min(width, 512)
    grad, squares = pl.pallas_call(
        functools.partial(grad_kernel, layout, n_all, tile),
        out_shape=(
            jax.ShapeDtypeStruct((feats, width), jnp.float32),
            jax.ShapeDtypeStruct((8 * n_all, 128), jnp.float32),
        ),
        in_specs=[VMEM] + [ANY] * len(flat),
        out_specs=(VMEM, VMEM),
        scratch_shapes=[
            pltpu.VMEM((tokens, width), jnp.bfloat16),
            pltpu.SemaphoreType.DMA((len(flat),)),
        ],
        compiler_params=pltpu.CompilerParams(vmem_limit_bytes=24 * MIB),
        name="gradient",
    )(acts_t, *flat)

    squares = lax.all_to_all(squares, both, 0, 0, tiled=True)

    step_rows = min(feats, 128)
    out_width = width * n_grp // n_tp
    block = lambda i: (i, 0)
    moment_new, second_new, partial_sum = pl.pallas_call(
        functools.partial(update_kernel, n_grp, feats * width * n_all),
        grid=(feats // step_rows,),
        out_shape=(
            jax.ShapeDtypeStruct(moment.shape, jnp.float32),
            jax.ShapeDtypeStruct(second.shape, jnp.float32),
            jax.ShapeDtypeStruct((slots * n_tp, out_width), jnp.bfloat16),
        ),
        in_specs=[
            pl.BlockSpec((8 * n_all, 128), lambda i: (0, 0)),
            pl.BlockSpec((step_rows, width), block),
            pl.BlockSpec((step_rows, width), block),
            pl.BlockSpec((step_rows, width), block),
            pl.BlockSpec((step_rows, width), block),
            pl.BlockSpec((slots * n_grp, step_rows), lambda i: (0, i)),
        ],
        out_specs=(
            pl.BlockSpec((step_rows, width), block),
            pl.BlockSpec((step_rows, width), block),
            pl.BlockSpec((slots * n_tp, out_width), lambda i: (0, 0)),
        ),
        scratch_shapes=[
            pltpu.VMEM((step_rows, width), jnp.bfloat16),
            pltpu.VMEM((slots * n_grp, width), jnp.float32),
        ],
        compiler_params=pltpu.CompilerParams(vmem_limit_bytes=24 * MIB),
        name="update",
    )(squares, grad, moment, second, weight, roll_all)

    swapped = lax.all_to_all(partial_sum, "tp", 0, 0, tiled=True)
    summed = jnp.sum(
        swapped.reshape(n_tp, slots, out_width).astype(jnp.float32), axis=0
    ).astype(jnp.bfloat16)
    halves = n_tp // n_grp
    home = [
        (g * n_tp + r * halves + h, r * n_tp + g * halves + h)
        for g in range(n_grp)
        for r in range(n_grp)
        for h in range(halves)
    ]
    arrived = lax.ppermute(summed, both, home)
    alive = lax.broadcasted_iota(jnp.int32, (slots, 1), 0) < live[0]
    prefill_out = jnp.where(alive, arrived, jnp.bfloat16(0.0))
    return (moment_new, second_new, prefill_out)


def solution(mesh):
    placed = (
        P("grp", "tp"),
        P("tp", "grp"),
        P("tp", "grp"),
        P("tp", "grp"),
        P("tp", "grp"),
        P("grp", "tp"),
        P("grp"),
    )
    return jax.shard_map(
        functools.partial(shards, mesh.shape["grp"], mesh.shape["tp"]),
        mesh=mesh,
        in_specs=placed,
        out_specs=(P("tp", "grp"), P("tp", "grp"), P("grp", "tp")),
        check_vma=False,
    )
```

```python
import functools

import jax
import jax.numpy as jnp
from jax import lax
from jax.experimental import pallas as pl
from jax.experimental.pallas import tpu as pltpu
from jax.sharding import PartitionSpec as P

E = 8192
D = 8192

beta_one = 0.9
beta_two = 0.95
learn_rate = 0.003
weight_decay = 0.1
adam_eps = 1e-08
step_count = 10

root_two = (1.0 - beta_two**step_count) ** 0.5
step_scale = learn_rate * root_two / (1.0 - beta_one**step_count)
eps_scaled = adam_eps * root_two
keep_scale = 1.0 - learn_rate * weight_decay


MIB = 1024 * 1024
ANY = pl.BlockSpec(memory_space=pl.ANY)
VMEM = pl.BlockSpec(memory_space=pltpu.VMEM)


def ring_order(count):
    return list(range(0, count, 2)) + list(range(1, count, 2))[::-1]


def ring_member(place, count):
    return jnp.where(place < (count + 1) // 2, 2 * place, 2 * (count - 1 - place) + 1)


def ring_place(member, count):
    return jnp.where(member % 2 == 0, member // 2, count - 1 - member // 2)


def ring_gather(pieces, axis, count):
    order = ring_order(count)
    ahead = [(order[i], order[(i + 1) % count]) for i in range(count)]
    back = [(b, a) for a, b in ahead]
    out, offsets = list(pieces), [0]
    left, right = list(pieces), list(pieces)
    for step in range(1, (count - 1) // 2 + 1):
        moved = []
        for i in range(2):
            moved.append(
                (lax.ppermute(left[i], axis, ahead), lax.ppermute(right[i], axis, back))
            )
        left, right = [m[0] for m in moved], [m[1] for m in moved]
        out += left + right
        offsets += [-step, step]
    if count % 2 == 0:
        out += [lax.ppermute(left[0], axis, ahead), lax.ppermute(right[1], axis, back)]
        offsets.append(count // 2)
    return out, offsets


def fold_gather(block, axis, count):
    out, masks = [block], [0]
    bit = count // 2
    while bit:
        swap = [(i, i ^ bit) for i in range(count)]
        out += [lax.ppermute(b, axis, swap) for b in out]
        masks += [m ^ bit for m in masks]
        bit //= 2
    return out, masks


def in_vmem(x):
    return pltpu.with_memory_space_constraint(x, pltpu.VMEM)


def in_hbm(x):
    return pltpu.with_memory_space_constraint(x, pltpu.HBM)


def pack_kernel(acts_ref, roll_ref, cot_ref, pack_ref, top_ref, low_ref, sems):
    learn, half = acts_ref.shape[0], top_ref.shape[0]
    slots = roll_ref.shape[0]
    copies = (
        pltpu.make_async_copy(cot_ref.at[pl.ds(0, half), :], top_ref, sems.at[0]),
        pltpu.make_async_copy(cot_ref.at[pl.ds(half, half), :], low_ref, sems.at[1]),
        pltpu.make_async_copy(acts_ref, pack_ref.at[pl.ds(0, learn), :], sems.at[2]),
        pltpu.make_async_copy(roll_ref, pack_ref.at[pl.ds(learn, slots), :], sems.at[3]),
    )
    for c in copies:
        c.start()
    for c in copies:
        c.wait()


def prep_kernel(offsets, masks, n_tp, rows, *refs):
    n_grp = len(masks)
    packs = refs[:n_grp]
    moment_ref, at_ref, roll_ref, moment_out, held, sem = refs[n_grp:]
    load = pltpu.make_async_copy(moment_ref, moment_out, sem)
    load.start()
    learn = held.shape[0] // n_grp
    slots = roll_ref.shape[0] // n_grp
    me = lax.axis_index("grp")
    for pack, mask in zip(packs, masks):
        owner = lax.bitwise_xor(me, mask)
        at = pl.ds(pl.multiple_of(owner * learn, learn), learn)
        held[at, :] = pack[0:learn, :]
        at = pl.ds(pl.multiple_of(owner * slots, slots), slots)
        roll_ref[at, :] = pack[learn : learn + slots, :]
    place = ring_place(lax.axis_index("tp"), n_tp)
    parts = []
    for off in offsets:
        member = ring_member(lax.rem(place + off + n_tp, n_tp), n_tp)
        parts.append(held[pl.ds(pl.multiple_of(member * rows, rows), rows), :])
    at_ref[...] = jnp.concatenate(parts, axis=0).T
    load.wait()


def grad_kernel(n_in, n_all, tile, *refs):
    at_ref = refs[0]
    pieces = refs[1 : 1 + n_in]
    second_ref, weight_ref = refs[1 + n_in : 3 + n_in]
    grad_ref, sq_ref, second_out, weight_out, sems = refs[3 + n_in :]
    loads = (
        pltpu.make_async_copy(second_ref, second_out, sems.at[0]),
        pltpu.make_async_copy(weight_ref, weight_out, sems.at[1]),
    )
    for load in loads:
        load.start()
    width = grad_ref.shape[1]
    total = jnp.zeros((8, 128), jnp.float32)
    for j in range(width // tile):
        cols = slice(j * tile, (j + 1) * tile)
        cot = jnp.concatenate([p[:, cols] for p in pieces], axis=0)
        part = jnp.dot(at_ref[...], cot, preferred_element_type=jnp.float32)
        grad_ref[:, cols] = part
        squares = part * part
        rows = jnp.sum(squares.reshape(-1, 8, tile), axis=0)
        for k in range(tile // 128):
            total = total + rows[:, k * 128 : (k + 1) * 128]
    for i in range(n_all):
        sq_ref[i * 8 : (i + 1) * 8, :] = total
    for load in loads:
        load.wait()


def update_kernel(
    n_grp, count, step_rows, sq_ref, grad_ref, moment_ref, second_ref, weight_ref,
    roll_ref, moment_out, second_out, part_ref, moments, seconds, fresh, sems,
):
    feats, width = grad_ref.shape
    ratio = jnp.full((16, 128), jnp.sum(sq_ref[...]) / count + 1e-06, jnp.float32)
    factor = jnp.minimum(1.0, 1.0 / jnp.sqrt(ratio))
    wide = min(width, 512)
    first = jnp.concatenate([(1.0 - beta_one) * factor] * (wide // 128), axis=1)
    other = jnp.concatenate([(1.0 - beta_two) * factor * factor] * (wide // 128), axis=1)

    def writes(i):
        at = pl.ds(pl.multiple_of(i * step_rows, step_rows), step_rows)
        return (
            pltpu.make_async_copy(moments.at[at, :], moment_out.at[at, :], sems.at[0]),
            pltpu.make_async_copy(seconds.at[at, :], second_out.at[at, :], sems.at[1]),
        )

    def body(i, _):
        for row in range(0, step_rows, 16):
            at = pl.ds(pl.multiple_of(i * step_rows + row, 16), 16)
            for j in range(width // wide):
                cols = slice(j * wide, (j + 1) * wide)
                grad = grad_ref[at, cols]
                moment = beta_one * moment_ref[at, cols] + first * grad
                second = beta_two * second_ref[at, cols] + (other * grad) * grad
                moments[at, cols] = moment
                seconds[at, cols] = second
                root = second * lax.rsqrt(second)
                move = (step_scale * moment) / (root + eps_scaled)
                old = weight_ref[at, cols].astype(jnp.float32)
                fresh[at, cols] = (keep_scale * old - move).astype(jnp.bfloat16)
        for w in writes(i):
            w.start()
        return 0

    lax.fori_loop(0, feats // step_rows, body, 0)
    out_width = part_ref.shape[1]
    slots = roll_ref.shape[0] // n_grp
    halves = width // out_width
    for h in range(halves):
        part = jnp.dot(
            roll_ref[...],
            fresh[:, h * out_width : (h + 1) * out_width],
            preferred_element_type=jnp.float32,
        ).astype(jnp.bfloat16)
        for r in range(n_grp):
            at = (r * halves + h) * slots
            part_ref[at : at + slots, :] = part[r * slots : (r + 1) * slots, :]
    pltpu.make_async_copy(moments, moment_out, sems.at[0]).wait()
    pltpu.make_async_copy(seconds, second_out, sems.at[1]).wait()


def shards(n_grp, n_tp, acts, cotangent, weight, moment, second, roll_acts, live):
    n_all = n_grp * n_tp
    feats, width = weight.shape
    slots = roll_acts.shape[0]
    learn = acts.shape[0]
    rows = cotangent.shape[0]
    tokens = rows * n_tp
    both = ("grp", "tp")

    pack, top, low = pl.pallas_call(
        pack_kernel,
        out_shape=(
            pltpu.VMEM((learn + slots, feats), jnp.bfloat16),
            pltpu.VMEM((rows // 2, width), jnp.bfloat16),
            pltpu.VMEM((rows // 2, width), jnp.bfloat16),
        ),
        in_specs=[ANY] * 3,
        out_specs=(VMEM,) * 3,
        scratch_shapes=[pltpu.SemaphoreType.DMA((4,))],
        compiler_params=pltpu.CompilerParams(vmem_limit_bytes=MIB),
        name="pack",
    )(in_hbm(acts), in_hbm(roll_acts), in_hbm(cotangent))
    packs, masks = fold_gather(pack, "grp", n_grp)
    cot_pieces, offsets = ring_gather((top, low), "tp", n_tp)
    acts_t, roll_all, moment = pl.pallas_call(
        functools.partial(prep_kernel, offsets, masks, n_tp, rows),
        out_shape=(
            pltpu.VMEM((feats, tokens), jnp.bfloat16),
            pltpu.VMEM((slots * n_grp, feats), jnp.bfloat16),
            pltpu.VMEM(moment.shape, jnp.float32),
        ),
        in_specs=[VMEM] * n_grp + [ANY],
        out_specs=(VMEM,) * 3,
        scratch_shapes=[
            pltpu.VMEM((tokens, feats), jnp.bfloat16),
            pltpu.SemaphoreType.DMA(()),
        ],
        compiler_params=pltpu.CompilerParams(vmem_limit_bytes=12 * MIB),
        name="prep",
    )(*[in_vmem(p) for p in packs], in_hbm(moment))

    tile = min(width, 512)
    n_in = len(cot_pieces)
    grad, squares, second, weight = pl.pallas_call(
        functools.partial(grad_kernel, n_in, n_all, tile),
        out_shape=(
            pltpu.VMEM((feats, width), jnp.float32),
            pltpu.VMEM((8 * n_all, 128), jnp.float32),
            pltpu.VMEM(second.shape, jnp.float32),
            pltpu.VMEM(weight.shape, jnp.bfloat16),
        ),
        in_specs=[VMEM] * (1 + n_in) + [ANY] * 2,
        out_specs=(VMEM,) * 4,
        scratch_shapes=[pltpu.SemaphoreType.DMA((2,))],
        compiler_params=pltpu.CompilerParams(vmem_limit_bytes=8 * MIB),
        name="gradient",
    )(
        in_vmem(acts_t), *[in_vmem(p) for p in cot_pieces],
        in_hbm(second), in_hbm(weight),
    )

    squares = lax.all_to_all(squares, both, 0, 0, tiled=True)

    out_width = width * n_grp // n_tp
    moment_new, second_new, partial_sum = pl.pallas_call(
        functools.partial(update_kernel, n_grp, feats * width * n_all, 32),
        out_shape=(
            pltpu.HBM((feats, width), jnp.float32),
            pltpu.HBM((feats, width), jnp.float32),
            pltpu.VMEM((slots * n_tp, out_width), jnp.bfloat16),
        ),
        in_specs=[VMEM] * 6,
        out_specs=(ANY, ANY, VMEM),
        scratch_shapes=[
            pltpu.VMEM((feats, width), jnp.float32),
            pltpu.VMEM((feats, width), jnp.float32),
            pltpu.VMEM((feats, width), jnp.bfloat16),
            pltpu.SemaphoreType.DMA((2,)),
        ],
        compiler_params=pltpu.CompilerParams(vmem_limit_bytes=24 * MIB),
        name="update",
    )(*[in_vmem(x) for x in (squares, grad, moment, second, weight, roll_all)])

    swapped = lax.all_to_all(partial_sum, "tp", 0, 0, tiled=True)
    summed = jnp.sum(
        swapped.reshape(n_tp, slots, out_width).astype(jnp.float32), axis=0
    ).astype(jnp.bfloat16)
    halves = n_tp // n_grp
    home = [
        (g * n_tp + r * halves + h, r * n_tp + g * halves + h)
        for g in range(n_grp)
        for r in range(n_grp)
        for h in range(halves)
    ]
    arrived = lax.ppermute(summed, both, home)
    alive = lax.broadcasted_iota(jnp.int32, (slots, 1), 0) < live[0]
    prefill_out = jnp.where(alive, arrived, jnp.bfloat16(0.0))
    return (moment_new, second_new, prefill_out)


def solution(mesh):
    placed = (
        P("grp", "tp"),
        P("tp", "grp"),
        P("tp", "grp"),
        P("tp", "grp"),
        P("tp", "grp"),
        P("grp", "tp"),
        P("grp"),
    )
    return jax.shard_map(
        functools.partial(shards, mesh.shape["grp"], mesh.shape["tp"]),
        mesh=mesh,
        in_specs=placed,
        out_specs=(P("tp", "grp"), P("tp", "grp"), P("grp", "tp")),
        check_vma=False,
    )
```
